32 devices in a mesh: groups: 2 (over y), dp: 16 (over z, x, core).
Axes of the slice: x: 2, y: 2, z: 4, core: 2. Of those that a mesh axis runs over, the one named last changes fastest.
Arguments:
- particles: bfloat16 [2048, 128, 128], P(('groups', 'dp')), parts along dimension 0, may hold values from -20 to 20
- refs: bfloat16 [128, 256, 128], P('dp', 'groups'), parts along dimension 1, may hold values from -0.5 to 0.5
- ctf_group: int32 [2048], P(('groups', 'dp')), parts along dimension 0, may hold values from 0 to 31, as said below
- defocus: float32 [64], P('groups'), parts along dimension 0, may hold values from 0.5 to 2
- class_prior: float32 [256], P('groups'), parts along dimension 0, may hold values from 0.25 to 4
- cycle_weight: float32 [64], replicated, may hold values from 0.5 to 2
Outputs:
- new_refs: float32 [128, 256, 128], P('dp', 'groups'), parts along dimension 1
- log_evidence: float32 [2048], P(('groups', 'dp')), parts along dimension 0
The draws below stay inside these ranges and needn't reach their ends.
There are 2 independent parts, one for each index of `groups`. The reference program is written for one: setup_inputs(seed, part) draws one part's arguments, and reference() takes and returns one part's arrays. A program takes and returns all parts, laid end to end along the dimension named above; an argument that names none is the same for every part. Nothing has to cross between parts.
Inputs may be any that keep to these rules, and one draw needn't show every extreme that they name: `ctf_group`: CTF groups follow the particle order: particle n belongs to group n * 32 // 1024 or the next one, capped at 31.
All inputs are finite; a program needn't handle non-finite values.
Results may differ from the reference program's by a relative error of at most 0.0045.
Values may be sent and summed in bfloat16 or wider, within the bound.
A program may use at most 64 MiB of HBM per device.

```python
import math
import jax
import jax.numpy as jnp
from jax import lax

M = 128
R = 64
K = 128
ROT = 36
G = 32
NP_DEV = 64
NALL = 1024


def ctf_values(defocus):
    radius = (jnp.arange(R, dtype=jnp.float32) + 1.0) / R
    phase = 20.0 * defocus[:, None] * radius[None, :] ** 2
    return -(0.995 * jnp.sin(phase) + 0.1 * jnp.cos(phase))


def shared_draw(key):
    key_ref = jax.random.fold_in(key, 11)
    key_label = jax.random.fold_in(key, 12)
    key_group = jax.random.fold_in(key, 13)
    key_focus = jax.random.fold_in(key, 14)
    key_noise = jax.random.fold_in(key, 15)
    index = jnp.arange(NALL, dtype=jnp.int32)
    base = index * G // NALL + jax.random.randint(key_group, (NALL,), 0, 2)
    ctf_group = jnp.minimum(base, G - 1).astype(jnp.int32)
    labels = jax.random.randint(key_label, (NALL,), 0, K)
    refs = jnp.clip(jax.random.normal(key_ref, (M, K, 2 * R), jnp.float32), -6.0, 6.0) / 64.0
    amplitude = jnp.full((NALL,), 4.0, jnp.float32)
    defocus = jnp.exp(jax.random.uniform(key_focus, (G,), jnp.float32, math.log(0.5), math.log(2.0)))
    noise = jnp.clip(jax.random.normal(key_noise, (NALL, M, 2 * R), jnp.float32), -6.0, 6.0)
    ctf = ctf_values(defocus)
    gain = jnp.concatenate([ctf, ctf], axis=1)[ctf_group]
    signal = jnp.take(jnp.transpose(refs, (1, 0, 2)), labels, axis=0)
    particles = amplitude[:, None, None] * gain[:, None, :] * signal + noise
    return (particles, refs, ctf_group, defocus)


def draw_particles(key, part):
    return shared_draw(key)[0].astype(jnp.bfloat16)


def draw_refs(key, part):
    return shared_draw(key)[1].astype(jnp.bfloat16)


def draw_ctf_group(key, part):
    return shared_draw(key)[2]


def draw_defocus(key, part):
    return shared_draw(key)[3]


def setup_inputs(seed: int = 0, part: int = 0) -> dict:
    keys = jax.random.split(jax.random.key(seed), 7)
    part_keys = jax.random.split(jax.random.fold_in(keys[6], part), 7)
    return {
        "particles": draw_particles(jax.random.fold_in(jax.random.fold_in(keys[6], part), 71), part),
        "refs": draw_refs(jax.random.fold_in(jax.random.fold_in(keys[6], part), 71), part),
        "ctf_group": draw_ctf_group(jax.random.fold_in(jax.random.fold_in(keys[6], part), 71), part),
        "defocus": draw_defocus(jax.random.fold_in(jax.random.fold_in(keys[6], part), 71), part),
        "class_prior": jnp.clip(jnp.exp(jax.random.uniform(part_keys[4], (K,), jnp.float32, math.log(0.25), math.log(4.0))), 0.25, 4.0),
        "cycle_weight": jnp.clip(jnp.exp(jax.random.uniform(keys[5], (R,), jnp.float32, math.log(0.5), math.log(2.0))), 0.5, 2.0),
    }


def ctf_table(defocus):
    radius = (jnp.arange(R, dtype=jnp.float32) + 1.0) / R
    phase = 20.0 * defocus[:, None] * radius[None, :] ** 2
    return -(0.995 * jnp.sin(phase) + 0.1 * jnp.cos(phase))


def angle_tables():
    harmonic = jnp.arange(M, dtype=jnp.float32)[:, None]
    turning = jnp.arange(ROT, dtype=jnp.float32)[None, :]
    theta = 2.0 * math.pi * harmonic * turning / ROT
    return jnp.cos(theta), jnp.sin(theta)


def reference(particles, refs, ctf_group, defocus, class_prior, cycle_weight):
    highest = lax.Precision.HIGHEST
    ctf = ctf_table(defocus)
    cos_table, sin_table = angle_tables()
    refs_wide = refs.astype(jnp.float32)
    energy = jnp.sum(refs_wide[:, :, :R] ** 2 + refs_wide[:, :, R:] ** 2, axis=0)
    quadratic = jnp.dot(cycle_weight[None, :] * ctf * ctf, energy.T, precision=highest)
    log_prior = jnp.log(class_prior)
    gain_table = jnp.concatenate([cycle_weight[None, :] * ctf, cycle_weight[None, :] * ctf], axis=1)

    def block_step(totals, inputs):
        numer, mass = totals
        images, labels = inputs
        onehot = (labels[:, None] == jnp.arange(G, dtype=jnp.int32)[None, :]).astype(jnp.float32)
        gain = jnp.dot(onehot, gain_table, precision=highest)
        weighted = (images.astype(jnp.float32) * gain[:, None, :]).astype(jnp.bfloat16)
        turned = jnp.concatenate([weighted[:, :, R:], -weighted[:, :, :R]], axis=2)
        wide_weighted = weighted.astype(jnp.float32)
        wide_turned = turned.astype(jnp.float32)
        cross_real = jnp.einsum('nmq,mkq->mnk', wide_weighted, refs_wide, precision=highest)
        cross_imag = jnp.einsum('nmq,mkq->mnk', wide_turned, refs_wide, precision=highest)
        corr = jnp.einsum('mnk,mj->nkj', cross_real, cos_table, precision=highest)
        corr = corr - jnp.einsum('mnk,mj->nkj', cross_imag, sin_table, precision=highest)
        norm_term = jnp.dot(onehot, quadratic, precision=highest)
        scores = corr - 0.5 * norm_term[:, :, None] + log_prior[None, :, None]
        flat = scores.reshape(scores.shape[0], K * ROT)
        top = jnp.max(flat, axis=1, keepdims=True)
        expo = jnp.exp(flat - top)
        total = jnp.sum(expo, axis=1, keepdims=True)
        posterior = (expo / total).reshape(scores.shape)
        evidence = top[:, 0] + jnp.log(total[:, 0])
        mass = mass + jnp.dot(onehot.T, jnp.sum(posterior, axis=2), precision=highest)
        post_real = jnp.einsum('nkj,mj->mnk', posterior, cos_table, precision=highest).astype(jnp.bfloat16)
        post_imag = jnp.einsum('nkj,mj->mnk', posterior, sin_table, precision=highest).astype(jnp.bfloat16)
        numer = numer + jnp.einsum('mnk,nmq->mkq', post_real.astype(jnp.float32), wide_weighted, precision=highest)
        numer = numer - jnp.einsum('mnk,nmq->mkq', post_imag.astype(jnp.float32), wide_turned, precision=highest)
        return (numer, mass), evidence

    blocks = NALL // NP_DEV
    images_all = particles.reshape(blocks, NP_DEV, M, 2 * R)
    labels_all = ctf_group.reshape(blocks, NP_DEV)
    start_numer = jnp.zeros((M, K, 2 * R), jnp.float32)
    start_mass = jnp.zeros((G, K), jnp.float32)
    (numer, mass), evidence = lax.scan(block_step, (start_numer, start_mass), (images_all, labels_all))
    denom = 1.0 + jnp.dot(mass.T, cycle_weight[None, :] * ctf * ctf, precision=highest)
    denom_wide = jnp.concatenate([denom, denom], axis=1)
    new_refs = numer / denom_wide[None, :, :]
    return new_refs, evidence.reshape(NALL)
```

```python
import functools
import math

import jax
import jax.numpy as jnp
from jax import lax
from jax.experimental import pallas as pl
from jax.experimental.pallas import tpu as pltpu
from jax.sharding import PartitionSpec as P

R = 64
ROT = 36
HALF = ROT // 2
NC = HALF + 1
G = 32
MESH = pl.DeviceIdType.MESH
HIGHEST = lax.Precision.HIGHEST


def ctf_table(defocus):
    radius = (jnp.arange(R, dtype=jnp.float32) + 1.0) / R
    phase = 20.0 * defocus[:, None] * radius[None, :] ** 2
    return -(0.995 * jnp.sin(phase) + 0.1 * jnp.cos(phase))


def peer_order(zn):
    return sorted(range(1, zn), key=lambda o: -min(o, zn - o))


def dev(index):
    return {"dp": index}


def gather_kernel(zn, refs_ref, wt_ref, out_ref, wpart_ref, local_sem, send, recv, wsend, wrecv):
    me = lax.axis_index("dp")
    z, x, c = me // 4, (me // 2) % 2, me % 2
    flip_x = z * 4 + (1 - x) * 2 + c
    flip_c = z * 4 + x * 2 + (1 - c)
    peers = [lax.rem(z + o, zn) * 4 + x * 2 + c for o in range(1, zn)]

    barrier = pltpu.get_barrier_semaphore()
    for p in peers + [flip_x, flip_c]:
        pl.semaphore_signal(barrier, inc=1, device_id=dev(p), device_id_type=MESH)
    pl.semaphore_wait(barrier, zn + 1)

    started = []

    def push(src, block, target, slot):
        copy = pltpu.make_async_remote_copy(
            src_ref=src,
            dst_ref=out_ref.at[block],
            send_sem=send.at[slot],
            recv_sem=recv.at[slot],
            device_id=dev(target),
            device_id_type=MESH,
        )
        copy.start()
        started.append(copy)
        return copy

    x0, c0 = zn - 1, 2 * zn - 1
    keep = pltpu.make_async_copy(refs_ref, out_ref.at[me], local_sem)
    keep.start()
    zc = {}
    for o in peer_order(zn):
        zc[o] = push(refs_ref, me, lax.rem(z + o, zn) * 4 + x * 2 + c, o - 1)
    xc = [push(refs_ref, me, flip_x, x0)]
    cc = [push(refs_ref, me, flip_c, c0)]
    wcopy = pltpu.make_async_remote_copy(
        src_ref=wt_ref.at[:, 1 - c],
        dst_ref=wpart_ref,
        send_sem=wsend,
        recv_sem=wrecv,
        device_id=dev(flip_c),
        device_id_type=MESH,
    )
    wcopy.start()
    order = sorted(range(1, zn), key=lambda o: min(o, zn - o))
    for i, o in enumerate(order):
        zc[o].wait_recv()
        block = lax.rem(z + zn - o, zn) * 4 + x * 2 + c
        xc.append(push(out_ref.at[block], block, flip_x, x0 + 1 + i))
        cc.append(push(out_ref.at[block], block, flip_c, c0 + 1 + i))
    for i, o in enumerate([0] + order):
        xc[i].wait_recv()
        block = lax.rem(z + zn - o, zn) * 4 + (1 - x) * 2 + c
        cc.append(push(out_ref.at[block], block, flip_c, c0 + zn + i))
    for copy in cc:
        copy.wait_recv()
    wcopy.wait_recv()
    for copy in started:
        copy.wait_send()
    wcopy.wait_send()
    keep.wait()


def dft_even_odd(even_in, odd_in, use_cos):
    f = math.cos if use_cos else math.sin

    def one(items, j):
        total = None
        for i, v in items:
            w = f(2.0 * math.pi * ((i * j) % ROT) / ROT)
            if abs(w) < 1e-12:
                continue
            if abs(w - 1.0) < 1e-12:
                term = v
            elif abs(w + 1.0) < 1e-12:
                term = -v
            else:
                term = v * jnp.float32(w)
            total = term if total is None else total + term
        return total

    count = HALF // 2 + 1
    return [one(even_in, j) for j in range(count)], [one(odd_in, j) for j in range(count)]


def half_transform(values, use_cos):
    even = [(i, v) for i, v in values.items() if i % 2 == 0]
    odd = [(i, v) for i, v in values.items() if i % 2 == 1]
    es, os_ = dft_even_odd(even, odd, use_cos)
    zero = jnp.zeros_like(next(iter(values.values())))
    out = {}
    for j in range(HALF // 2 + 1):
        e = zero if es[j] is None else es[j]
        o = zero if os_[j] is None else os_[j]
        out[j] = e + o
        out[HALF - j] = (e - o) if use_cos else (o - e)
    return out


def estep_kernel(refs_ref, wt_ref, anorm_ref, prior_ref, hot_ref, pp_ref, ev_ref, mass_ref, cres, energy, bias, psum):
    m_all = refs_ref.shape[0]
    n = wt_ref.shape[1]
    q = wt_ref.shape[2]
    lane = lax.broadcasted_iota(jnp.int32, (n, q), 1)
    sign = jnp.where(lane < R, jnp.float32(1.0), jnp.float32(-1.0))
    energy[...] = jnp.zeros_like(energy)

    def residue(r, count):
        acc = None
        sq = None
        for t in range(count):
            m = r + ROT * t
            w = wt_ref[m]
            turned = (pltpu.roll(w.astype(jnp.float32), R, 1) * sign).astype(jnp.bfloat16)
            both = jnp.concatenate([w, turned], axis=0)
            ref = refs_ref[m]
            part = lax.dot_general(
                both, ref, (((1,), (1,)), ((), ())), preferred_element_type=jnp.float32
            )
            acc = part if acc is None else acc + part
            wide = ref.astype(jnp.float32)
            sq = wide * wide if sq is None else sq + wide * wide
        cres[r] = acc
        energy[...] += sq

    full, extra = m_all // ROT, m_all % ROT
    if extra:
        pl.loop(0, extra)(lambda r: residue(r, full + 1))
    pl.loop(extra, ROT)(lambda r: residue(r, full))

    norm = lax.dot_general(
        anorm_ref[...], energy[...], (((1,), (1,)), ((), ())),
        preferred_element_type=jnp.float32, precision=HIGHEST,
    )
    bias[...] = prior_ref[...] - norm

    rows = 16

    @pl.loop(0, n // rows)
    def _(i):
        at = pl.ds(pl.multiple_of(i * rows, rows), rows)
        at_im = pl.ds(pl.multiple_of(n + i * rows, rows), rows)
        a = {0: cres[0, at, :], HALF: cres[HALF, at, :]}
        b = {}
        for r in range(1, HALF):
            a[r] = cres[r, at, :] + cres[ROT - r, at, :]
            b[r] = cres[r, at_im, :] - cres[ROT - r, at_im, :]
        cosine = half_transform(a, True)
        sine = half_transform(b, False)
        add = bias[at, :]
        scores = {}
        for j in range(NC):
            base = cosine[j] + add
            if j in (0, HALF):
                scores[j] = base
            else:
                scores[j] = base - sine[j]
                scores[ROT - j] = base + sine[j]
        top = scores[0]
        for j in range(1, ROT):
            top = jnp.maximum(top, scores[j])
        top = jnp.max(top, axis=1, keepdims=True)
        total = None
        expo = {}
        for j in range(ROT):
            expo[j] = jnp.exp(scores[j] - top)
            total = expo[j] if total is None else total + expo[j]
        norm_total = jnp.sum(total, axis=1, keepdims=True)
        ev_ref[at, :] = jnp.broadcast_to(top + jnp.log(norm_total), (rows, 128))
        inv = 1.0 / norm_total
        psum[at, :] = total * inv
        u = {0: expo[0] * inv, HALF: expo[HALF] * inv}
        v = {}
        for j in range(1, HALF):
            u[j] = (expo[j] + expo[ROT - j]) * inv
            v[j] = (expo[j] - expo[ROT - j]) * inv
        real = half_transform(u, True)
        imag = half_transform(v, False)
        for r in range(NC):
            pp_ref[r, at, :] = real[r].astype(jnp.bfloat16)
            pp_ref[NC + r, at, :] = imag[r].astype(jnp.bfloat16)

    mass_ref[...] = lax.dot_general(
        hot_ref[...], psum[...], (((1,), (0,)), ((), ())),
        preferred_element_type=jnp.float32, precision=HIGHEST,
    )


def mstep_kernel(zn, dp, pp_ref, wt_ref, wpart_ref, mass_ref, table_ref, out_ref,
                 pbuf, pt, xsend, xrecv, acc, zsend, zrecv, mslots,
                 psend_s, psend_r, xs, xr, zs, zr, ms, mr):
    me = lax.axis_index("dp")
    z, x, c = me // 4, (me // 2) % 2, me % 2
    flip_x = z * 4 + (1 - x) * 2 + c
    flip_c = z * 4 + x * 2 + (1 - c)
    mb, k, q = out_ref.shape

    barrier = pltpu.get_barrier_semaphore()
    for o in range(1, dp):
        pl.semaphore_signal(barrier, inc=1, device_id=dev(lax.rem(me + o, dp)), device_id_type=MESH)
    pl.semaphore_wait(barrier, dp - 1)

    pcopy = pltpu.make_async_remote_copy(
        src_ref=pp_ref, dst_ref=pbuf, send_sem=psend_s, recv_sem=psend_r,
        device_id=dev(flip_c), device_id_type=MESH,
    )
    pcopy.start()
    mcopies = []
    for o in range(1, dp):
        copy = pltpu.make_async_remote_copy(
            src_ref=mass_ref, dst_ref=mslots.at[me], send_sem=ms.at[o], recv_sem=mr.at[o],
            device_id=dev(lax.rem(me + o, dp)), device_id_type=MESH,
        )
        copy.start()
        mcopies.append(copy)
    mslots[me] = mass_ref[...]
    pcopy.wait()

    @pl.loop(0, 2 * NC)
    def _(i):
        pt[i] = jnp.concatenate([pp_ref[i], pbuf[i]], axis=0).T

    lane = lax.broadcasted_iota(jnp.int32, (k, q), 1)
    mask = jnp.where(lane < R, jnp.float32(-1.0), jnp.float32(1.0))

    def numer(zx, i):
        m = (zx * 2 + c) * mb + i
        r = lax.rem(m, ROT)
        rr = jnp.minimum(r, ROT - r)
        s = jnp.where(r > HALF, -1, 1).astype(jnp.float32)
        w = jnp.concatenate([wt_ref[zx, c, i], wpart_ref[zx, i]], axis=0)
        u = jnp.dot(pt[rr], w, preferred_element_type=jnp.float32)
        v = jnp.dot(pt[NC + rr], w, preferred_element_type=jnp.float32)
        return u + pltpu.roll(v, R, 1) * (mask * s)

    order = peer_order(zn) + [0]
    xcopies = []
    for o in order:
        zz = lax.rem(z + o, zn)

        @pl.loop(0, mb)
        def _(i):
            xsend[o, i] = numer(zz * 2 + 1 - x, i).astype(jnp.bfloat16)

        copy = pltpu.make_async_remote_copy(
            src_ref=xsend.at[o], dst_ref=xrecv.at[o], send_sem=xs.at[o], recv_sem=xr.at[o],
            device_id=dev(flip_x), device_id_type=MESH,
        )
        copy.start()
        xcopies.append(copy)

    zcopies = []
    for o, xcopy in zip(order, xcopies):
        zz = lax.rem(z + o, zn)

        @pl.loop(0, mb)
        def _(i):
            acc[i] = numer(zz * 2 + x, i)

        xcopy.wait_recv()
        if o:
            @pl.loop(0, mb)
            def _(i):
                zsend[o, i] = (acc[i] + xrecv[o, i].astype(jnp.float32)).astype(jnp.bfloat16)

            copy = pltpu.make_async_remote_copy(
                src_ref=zsend.at[o], dst_ref=zrecv.at[o], send_sem=zs.at[o], recv_sem=zr.at[o],
                device_id=dev(zz * 4 + x * 2 + c), device_id_type=MESH,
            )
            copy.start()
            zcopies.append(copy)
    for copy in mcopies:
        copy.wait_recv()
    wide = mslots[...].reshape(dp * mslots.shape[1], k)
    denom = 1.0 + lax.dot_general(
        wide, table_ref[...], (((0,), (0,)), ((), ())),
        preferred_element_type=jnp.float32, precision=HIGHEST,
    )
    inv = 1.0 / denom
    for copy in zcopies:
        copy.wait_recv()

    @pl.loop(0, mb)
    def _(i):
        total = acc[i] + xrecv[0, i].astype(jnp.float32)
        for o in range(1, zn):
            total = total + zrecv[o, i].astype(jnp.float32)
        out_ref[i] = total * inv

    for copy in xcopies + zcopies + mcopies:
        copy.wait_send()


def shards(dp, particles, refs, ctf_group, defocus, class_prior, cycle_weight):
    n, m_all, q = particles.shape
    mb, k, _ = refs.shape
    zn = dp // 4
    nall = n * dp
    me = lax.axis_index("dp")
    ctf = ctf_table(defocus)
    onehot = (ctf_group[:, None] == jnp.arange(G, dtype=jnp.int32)[None, :]).astype(jnp.float32)
    gain_table = cycle_weight[None, :] * ctf
    power = gain_table * ctf
    picked = jnp.dot(onehot, jnp.concatenate([gain_table, gain_table, power, power], axis=1), precision=HIGHEST)
    gain, anorm = picked[:, :q], 0.5 * picked[:, q:]
    weighted = (particles.astype(jnp.float32) * gain[:, None, :]).astype(jnp.bfloat16)
    wt = jnp.transpose(weighted, (1, 0, 2))
    wt6 = wt.reshape(dp // 2, 2, mb, n, q)

    window = -(-((n * G) // nall + 2) // 8) * 8
    starts = jnp.arange(dp, dtype=jnp.int32) * n * G // nall
    rel = jnp.arange(window, dtype=jnp.int32)
    hot = (ctf_group[None, :] == (starts[me] + rel)[:, None]).astype(jnp.float32)
    rows = (starts[:, None] + rel[None, :]).reshape(-1)
    table = jnp.where((rows < G)[:, None], jnp.concatenate([power, power], axis=1)[jnp.minimum(rows, G - 1)], 0.0)

    vmem = pl.BlockSpec(memory_space=pltpu.VMEM)
    hbm = pl.BlockSpec(memory_space=pl.ANY)
    copies = 4 * zn - 1
    all_refs, wpart = pl.pallas_call(
        functools.partial(gather_kernel, zn),
        out_shape=(
            jax.ShapeDtypeStruct((dp, mb, k, q), jnp.bfloat16),
            jax.ShapeDtypeStruct((dp // 2, mb, n, q), jnp.bfloat16),
        ),
        in_specs=[vmem, hbm],
        out_specs=(hbm, hbm),
        scratch_shapes=[
            pltpu.SemaphoreType.DMA,
            pltpu.SemaphoreType.DMA((copies,)),
            pltpu.SemaphoreType.DMA((copies,)),
            pltpu.SemaphoreType.DMA,
            pltpu.SemaphoreType.DMA,
        ],
        compiler_params=pltpu.CompilerParams(collective_id=0, has_side_effects=True),
        name="gather",
    )(refs, wt6)

    pp, ev, mass = pl.pallas_call(
        estep_kernel,
        out_shape=(
            jax.ShapeDtypeStruct((2 * NC, n, k), jnp.bfloat16),
            jax.ShapeDtypeStruct((n, 128), jnp.float32),
            jax.ShapeDtypeStruct((window, k), jnp.float32),
        ),
        in_specs=[vmem] * 5,
        out_specs=(vmem,) * 3,
        scratch_shapes=[
            pltpu.VMEM((ROT, 2 * n, k), jnp.float32),
            pltpu.VMEM((k, q), jnp.float32),
            pltpu.VMEM((n, k), jnp.float32),
            pltpu.VMEM((n, k), jnp.float32),
        ],
        name="estep",
    )(all_refs.reshape(m_all, k, q), wt, anorm, jnp.log(class_prior)[None, :], hot)

    sem = pltpu.SemaphoreType.DMA
    new_refs = pl.pallas_call(
        functools.partial(mstep_kernel, zn, dp),
        out_shape=jax.ShapeDtypeStruct((mb, k, q), jnp.float32),
        in_specs=[vmem] * 5,
        out_specs=vmem,
        scratch_shapes=[
            pltpu.VMEM((2 * NC, n, k), jnp.bfloat16),
            pltpu.VMEM((2 * NC, k, 2 * n), jnp.bfloat16),
            pltpu.VMEM((zn, mb, k, q), jnp.bfloat16),
            pltpu.VMEM((zn, mb, k, q), jnp.bfloat16),
            pltpu.VMEM((mb, k, q), jnp.float32),
            pltpu.VMEM((zn, mb, k, q), jnp.bfloat16),
            pltpu.VMEM((zn, mb, k, q), jnp.bfloat16),
            pltpu.VMEM((dp, window, k), jnp.float32),
            sem, sem,
            sem((zn,)), sem((zn,)), sem((zn,)), sem((zn,)), sem((dp,)), sem((dp,)),
        ],
        compiler_params=pltpu.CompilerParams(collective_id=1, has_side_effects=True),
        name="mstep",
    )(pp, wt6, wpart, mass, table)
    return (new_refs, ev[:, 0])


def solution(mesh):
    in_specs = (
        P(("groups", "dp"), None, None),
        P("dp", "groups", None),
        P(("groups", "dp")),
        P("groups"),
        P("groups"),
        P(),
    )
    out_specs = (P("dp", "groups", None), P(("groups", "dp")))
    return jax.shard_map(
        functools.partial(shards, mesh.shape["dp"]),
        mesh=mesh, in_specs=in_specs, out_specs=out_specs, check_vma=False,
    )
```

```python
import functools
import math

import jax
import jax.numpy as jnp
from jax import lax
from jax.experimental import pallas as pl
from jax.experimental.pallas import tpu as pltpu
from jax.sharding import PartitionSpec as P

R = 64
ROT = 36
HALF = ROT // 2
NC = HALF + 1
G = 32
MESH = pl.DeviceIdType.MESH
HIGHEST = lax.Precision.HIGHEST


def dev(index):
    return {"dp": index}


def ring_steps(zn):
    plus = zn // 2
    minus = zn - 1 - plus
    steps = []
    for d in range(1, plus + 1):
        steps.append((1, d))
        if d <= minus:
            steps.append((-1, d))
    return steps


def gather_kernel(zn, dp, window, refs_ref, part_ref, col_ref, row_ref, focus_ref, cw_ref,
                  out_ref, wt_ref, wpart_ref, anorm_ref, hot_ref, table_ref,
                  local_sem, send, recv, wsend, wrecv):
    me = lax.axis_index("dp")
    z, x, c = me // 4, (me // 2) % 2, me % 2
    flip_x = z * 4 + (1 - x) * 2 + c
    flip_c = z * 4 + x * 2 + (1 - c)
    steps = ring_steps(zn)
    reach = {1: zn // 2, -1: zn - 1 - zn // 2}
    beside = {s: lax.rem(z + zn + s, zn) * 4 + x * 2 + c for s in {d for d, _ in steps}}
    n, m_all, q = part_ref.shape
    mb = refs_ref.shape[0]
    nall = n * dp

    barrier = pltpu.get_barrier_semaphore()
    greet = list(beside.values()) + [flip_x, flip_c]
    for p in greet:
        pl.semaphore_signal(barrier, inc=1, device_id=dev(p), device_id_type=MESH)
    pl.semaphore_wait(barrier, len(greet))

    started = []

    def push(src, block, target, slot):
        copy = pltpu.make_async_remote_copy(
            src_ref=src,
            dst_ref=out_ref.at[block],
            send_sem=send.at[slot],
            recv_sem=recv.at[slot],
            device_id=dev(target),
            device_id_type=MESH,
        )
        copy.start()
        started.append(copy)
        return copy

    x0, c0 = zn - 1, 2 * zn - 1
    slot_of = {step: i for i, step in enumerate(steps)}
    zc = {}
    for s in beside:
        zc[(s, 1)] = push(refs_ref, me, beside[s], slot_of[(s, 1)])
    xc = [push(refs_ref, me, flip_x, x0)]
    cc = [push(refs_ref, me, flip_c, c0)]
    keep = pltpu.make_async_copy(refs_ref, out_ref.at[me], local_sem)
    keep.start()

    lane = lax.broadcasted_iota(jnp.int32, (G, q), 1)
    radius = (jnp.where(lane < R, lane, lane - R).astype(jnp.float32) + 1.0) / R
    phase = 20.0 * focus_ref[...] * (radius * radius)
    ctf = -(0.995 * jnp.sin(phase) + 0.1 * jnp.cos(phase))
    cw = jnp.concatenate([cw_ref[...], cw_ref[...]], axis=1)
    gain_table = cw * ctf
    power = gain_table * ctf

    def dot(a, b):
        return jnp.dot(a, b, precision=HIGHEST, preferred_element_type=jnp.float32)

    onehot = (col_ref[...] == lax.broadcasted_iota(jnp.int32, (n, G), 1)).astype(jnp.float32)
    gain = dot(onehot, gain_table)
    anorm_ref[...] = 0.5 * dot(onehot, power)
    start = (me * (n * G)) // nall
    hot_ref[...] = (
        row_ref[...] == lax.broadcasted_iota(jnp.int32, (window, n), 0) + start
    ).astype(jnp.float32)
    below = lax.broadcasted_iota(jnp.int32, (window, G), 0) - lax.broadcasted_iota(jnp.int32, (window, G), 1)
    for d in range(dp):
        pick = (below == -(d * n * G // nall)).astype(jnp.float32)
        table_ref[d * window:(d + 1) * window, :] = dot(pick, power)

    chunk = 16

    @pl.loop(0, m_all // chunk)
    def _(i):
        at = pl.ds(pl.multiple_of(i * chunk, chunk), chunk)
        wide = part_ref[:, at, :].astype(jnp.float32) * gain[:, None, :]
        wt_ref[at] = jnp.swapaxes(wide, 0, 1).astype(jnp.bfloat16)

    for i, (s, d) in enumerate(steps):
        zc[(s, d)].wait_recv()
        block = lax.rem(z + zn - s * d, zn) * 4 + x * 2 + c
        if d < reach[s]:
            zc[(s, d + 1)] = push(out_ref.at[block], block, beside[s], slot_of[(s, d + 1)])
        xc.append(push(out_ref.at[block], block, flip_x, x0 + 1 + i))
        cc.append(push(out_ref.at[block], block, flip_c, c0 + 1 + i))
        if i == 0:
            wcopies = []
            for b in range(dp // 2):
                copy = pltpu.make_async_remote_copy(
                    src_ref=wt_ref.at[pl.ds((2 * b + 1 - c) * mb, mb)],
                    dst_ref=wpart_ref.at[b],
                    send_sem=wsend.at[b],
                    recv_sem=wrecv.at[b],
                    device_id=dev(flip_c),
                    device_id_type=MESH,
                )
                copy.start()
                wcopies.append(copy)
    for i, (s, d) in enumerate([(1, 0)] + steps):
        xc[i].wait_recv()
        block = lax.rem(z + zn - s * d, zn) * 4 + (1 - x) * 2 + c
        cc.append(push(out_ref.at[block], block, flip_c, c0 + zn + i))
    for copy in cc + wcopies:
        copy.wait_recv()
    for copy in started + wcopies:
        copy.wait_send()
    keep.wait()


def dft_even_odd(even_in, odd_in, use_cos):
    f = math.cos if use_cos else math.sin

    def one(items, j):
        total = None
        for i, v in items:
            w = f(2.0 * math.pi * ((i * j) % ROT) / ROT)
            if abs(w) < 1e-12:
                continue
            if abs(w - 1.0) < 1e-12:
                term = v
            elif abs(w + 1.0) < 1e-12:
                term = -v
            else:
                term = v * jnp.float32(w)
            total = term if total is None else total + term
        return total

    count = HALF // 2 + 1
    return [one(even_in, j) for j in range(count)], [one(odd_in, j) for j in range(count)]


def half_transform(values, use_cos):
    even = [(i, v) for i, v in values.items() if i % 2 == 0]
    odd = [(i, v) for i, v in values.items() if i % 2 == 1]
    es, os_ = dft_even_odd(even, odd, use_cos)
    zero = jnp.zeros_like(next(iter(values.values())))
    out = {}
    for j in range(HALF // 2 + 1):
        e = zero if es[j] is None else es[j]
        o = zero if os_[j] is None else os_[j]
        out[j] = e + o
        out[HALF - j] = (e - o) if use_cos else (o - e)
    return out


def estep_kernel(refs_ref, wt_ref, anorm_ref, prior_ref, hot_ref, pp_ref, ev_ref, mass_ref, cres, energy, bias, psum):
    m_all = refs_ref.shape[0]
    n = wt_ref.shape[1]
    q = wt_ref.shape[2]
    lane = lax.broadcasted_iota(jnp.int32, (n, q), 1)
    sign = jnp.where(lane < R, jnp.float32(1.0), jnp.float32(-1.0))
    energy[...] = jnp.zeros_like(energy)

    def residue(r, count):
        acc = None
        sq = None
        for t in range(count):
            m = r + ROT * t
            w = wt_ref[m]
            turned = (pltpu.roll(w.astype(jnp.float32), R, 1) * sign).astype(jnp.bfloat16)
            both = jnp.concatenate([w, turned], axis=0)
            ref = refs_ref[m]
            part = lax.dot_general(
                both, ref, (((1,), (1,)), ((), ())), preferred_element_type=jnp.float32
            )
            acc = part if acc is None else acc + part
            wide = ref.astype(jnp.float32)
            sq = wide * wide if sq is None else sq + wide * wide
        cres[r] = acc
        energy[...] += sq

    full, extra = m_all // ROT, m_all % ROT
    if extra:
        pl.loop(0, extra)(lambda r: residue(r, full + 1))
    pl.loop(extra, ROT)(lambda r: residue(r, full))

    norm = lax.dot_general(
        anorm_ref[...], energy[...], (((1,), (1,)), ((), ())),
        preferred_element_type=jnp.float32, precision=HIGHEST,
    )
    bias[...] = jnp.log(prior_ref[...]) - norm

    rows = 16

    @pl.loop(0, n // rows)
    def _(i):
        at = pl.ds(pl.multiple_of(i * rows, rows), rows)
        at_im = pl.ds(pl.multiple_of(n + i * rows, rows), rows)
        a = {0: cres[0, at, :], HALF: cres[HALF, at, :]}
        b = {}
        for r in range(1, HALF):
            a[r] = cres[r, at, :] + cres[ROT - r, at, :]
            b[r] = cres[r, at_im, :] - cres[ROT - r, at_im, :]
        cosine = half_transform(a, True)
        sine = half_transform(b, False)
        add = bias[at, :]
        scores = {}
        for j in range(NC):
            base = cosine[j] + add
            if j in (0, HALF):
                scores[j] = base
            else:
                scores[j] = base - sine[j]
                scores[ROT - j] = base + sine[j]
        top = scores[0]
        for j in range(1, ROT):
            top = jnp.maximum(top, scores[j])
        top = jnp.max(top, axis=1, keepdims=True)
        total = None
        expo = {}
        for j in range(ROT):
            expo[j] = jnp.exp(scores[j] - top)
            total = expo[j] if total is None else total + expo[j]
        norm_total = jnp.sum(total, axis=1, keepdims=True)
        ev_ref[at, :] = jnp.broadcast_to(top + jnp.log(norm_total), (rows, 128))
        inv = 1.0 / norm_total
        psum[at, :] = total * inv
        u = {0: expo[0] * inv, HALF: expo[HALF] * inv}
        v = {}
        for j in range(1, HALF):
            u[j] = (expo[j] + expo[ROT - j]) * inv
            v[j] = (expo[j] - expo[ROT - j]) * inv
        real = half_transform(u, True)
        imag = half_transform(v, False)
        for r in range(NC):
            pp_ref[r, at, :] = real[r].astype(jnp.bfloat16)
            pp_ref[NC + r, at, :] = imag[r].astype(jnp.bfloat16)

    mass_ref[...] = lax.dot_general(
        hot_ref[...], psum[...], (((1,), (0,)), ((), ())),
        preferred_element_type=jnp.float32, precision=HIGHEST,
    )


def mstep_kernel(zn, dp, pp_ref, wt_ref, wpart_ref, mass_ref, table_ref, out_ref,
                 pbuf, pt, xsend, xrecv, acc, zsend, zrecv, mslots,
                 psend_s, psend_r, xs, xr, zs, zr, ms, mr):
    me = lax.axis_index("dp")
    z, x, c = me // 4, (me // 2) % 2, me % 2
    flip_x = z * 4 + (1 - x) * 2 + c
    flip_c = z * 4 + x * 2 + (1 - c)
    mb, k, q = out_ref.shape

    barrier = pltpu.get_barrier_semaphore()
    for o in range(1, dp):
        pl.semaphore_signal(barrier, inc=1, device_id=dev(lax.rem(me + o, dp)), device_id_type=MESH)
    pl.semaphore_wait(barrier, dp - 1)

    pcopy = pltpu.make_async_remote_copy(
        src_ref=pp_ref, dst_ref=pbuf, send_sem=psend_s, recv_sem=psend_r,
        device_id=dev(flip_c), device_id_type=MESH,
    )
    pcopy.start()
    mcopies = []
    for o in range(1, dp):
        copy = pltpu.make_async_remote_copy(
            src_ref=mass_ref, dst_ref=mslots.at[me], send_sem=ms.at[o], recv_sem=mr.at[o],
            device_id=dev(lax.rem(me + o, dp)), device_id_type=MESH,
        )
        copy.start()
        mcopies.append(copy)
    mslots[me] = mass_ref[...]
    pcopy.wait()

    @pl.loop(0, 2 * NC)
    def _(i):
        pt[i] = jnp.concatenate([pp_ref[i], pbuf[i]], axis=0).T

    lane = lax.broadcasted_iota(jnp.int32, (k, q), 1)
    mask = jnp.where(lane < R, jnp.float32(-1.0), jnp.float32(1.0))

    def numer(zx, i):
        m = (zx * 2 + c) * mb + i
        r = lax.rem(m, ROT)
        rr = jnp.minimum(r, ROT - r)
        s = jnp.where(r > HALF, -1, 1).astype(jnp.float32)
        w = jnp.concatenate([wt_ref[m], wpart_ref[zx, i]], axis=0)
        u = jnp.dot(pt[rr], w, preferred_element_type=jnp.float32)
        v = jnp.dot(pt[NC + rr], w, preferred_element_type=jnp.float32)
        return u + pltpu.roll(v, R, 1) * (mask * s)

    steps = ring_steps(zn)
    reach = {1: zn // 2, -1: zn - 1 - zn // 2}
    order = [((s * (reach[s] + 1 - d)) % zn, s, d) for s, d in steps] + [(0, 0, 0)]
    xcopies = []
    for o, _, _ in order:
        zz = lax.rem(z + o, zn)

        @pl.loop(0, mb)
        def _(i):
            xsend[o, i] = numer(zz * 2 + 1 - x, i).astype(jnp.bfloat16)

        copy = pltpu.make_async_remote_copy(
            src_ref=xsend.at[o], dst_ref=xrecv.at[o], send_sem=xs.at[o], recv_sem=xr.at[o],
            device_id=dev(flip_x), device_id_type=MESH,
        )
        copy.start()
        xcopies.append(copy)

    zcopies = {}
    last = []
    for j, ((o, s, d), xcopy) in enumerate(zip(order, xcopies)):
        zz = lax.rem(z + o, zn)

        @pl.loop(0, mb)
        def _(i):
            acc[i] = numer(zz * 2 + x, i)

        xcopy.wait_recv()
        if o:
            before = None
            if d > 1:
                before, got = zcopies[(s, d - 1)]
                got.wait_recv()

            @pl.loop(0, mb)
            def _(i):
                total = acc[i] + xrecv[o, i].astype(jnp.float32)
                if before is not None:
                    total = total + zrecv[before, i].astype(jnp.float32)
                zsend[j, i] = total.astype(jnp.bfloat16)

            copy = pltpu.make_async_remote_copy(
                src_ref=zsend.at[j], dst_ref=zrecv.at[j], send_sem=zs.at[j], recv_sem=zr.at[j],
                device_id=dev(lax.rem(z + zn + s, zn) * 4 + x * 2 + c), device_id_type=MESH,
            )
            copy.start()
            zcopies[(s, d)] = (j, copy)
            if d == reach[s]:
                last.append((j, copy))
    for copy in mcopies:
        copy.wait_recv()
    wide = mslots[...].reshape(dp * mslots.shape[1], k)
    denom = 1.0 + lax.dot_general(
        wide, table_ref[...], (((0,), (0,)), ((), ())),
        preferred_element_type=jnp.float32, precision=HIGHEST,
    )
    inv = 1.0 / denom
    for _, copy in last:
        copy.wait_recv()

    @pl.loop(0, mb)
    def _(i):
        total = acc[i] + xrecv[0, i].astype(jnp.float32)
        for j, _ in last:
            total = total + zrecv[j, i].astype(jnp.float32)
        out_ref[i] = total * inv

    for copy in xcopies + [copy for _, copy in zcopies.values()] + mcopies:
        copy.wait_send()


def shards(dp, particles, refs, ctf_group, defocus, class_prior, cycle_weight):
    n, m_all, q = particles.shape
    mb, k, _ = refs.shape
    zn = dp // 4
    nall = n * dp
    window = -(-((n * G) // nall + 2) // 8) * 8

    vmem = pl.BlockSpec(memory_space=pltpu.VMEM)
    hbm = pl.BlockSpec(memory_space=pl.ANY)
    copies = 4 * zn - 1
    sem = pltpu.SemaphoreType.DMA
    all_refs, wt, wpart, anorm, hot, table = pl.pallas_call(
        functools.partial(gather_kernel, zn, dp, window),
        out_shape=(
            jax.ShapeDtypeStruct((dp, mb, k, q), jnp.bfloat16),
            jax.ShapeDtypeStruct((m_all, n, q), jnp.bfloat16),
            jax.ShapeDtypeStruct((dp // 2, mb, n, q), jnp.bfloat16),
            jax.ShapeDtypeStruct((n, q), jnp.float32),
            jax.ShapeDtypeStruct((window, n), jnp.float32),
            jax.ShapeDtypeStruct((dp * window, q), jnp.float32),
        ),
        in_specs=[vmem] * 6,
        out_specs=(hbm, vmem, hbm, vmem, vmem, vmem),
        scratch_shapes=[
            sem, sem((copies,)), sem((copies,)), sem((dp // 2,)), sem((dp // 2,)),
        ],
        compiler_params=pltpu.CompilerParams(collective_id=0, has_side_effects=True),
        name="gather",
    )(refs, particles, ctf_group[:, None], ctf_group[None, :], defocus[:, None], cycle_weight[None, :])

    pp, ev, mass = pl.pallas_call(
        estep_kernel,
        out_shape=(
            jax.ShapeDtypeStruct((2 * NC, n, k), jnp.bfloat16),
            jax.ShapeDtypeStruct((n, 128), jnp.float32),
            jax.ShapeDtypeStruct((window, k), jnp.float32),
        ),
        in_specs=[vmem] * 5,
        out_specs=(vmem,) * 3,
        scratch_shapes=[
            pltpu.VMEM((ROT, 2 * n, k), jnp.float32),
            pltpu.VMEM((k, q), jnp.float32),
            pltpu.VMEM((n, k), jnp.float32),
            pltpu.VMEM((n, k), jnp.float32),
        ],
        name="estep",
    )(all_refs.reshape(m_all, k, q), wt, anorm, class_prior[None, :], hot)

    new_refs = pl.pallas_call(
        functools.partial(mstep_kernel, zn, dp),
        out_shape=jax.ShapeDtypeStruct((mb, k, q), jnp.float32),
        in_specs=[vmem] * 5,
        out_specs=vmem,
        scratch_shapes=[
            pltpu.VMEM((2 * NC, n, k), jnp.bfloat16),
            pltpu.VMEM((2 * NC, k, 2 * n), jnp.bfloat16),
            pltpu.VMEM((zn, mb, k, q), jnp.bfloat16),
            pltpu.VMEM((zn, mb, k, q), jnp.bfloat16),
            pltpu.VMEM((mb, k, q), jnp.float32),
            pltpu.VMEM((zn, mb, k, q), jnp.bfloat16),
            pltpu.VMEM((zn, mb, k, q), jnp.bfloat16),
            pltpu.VMEM((dp, window, k), jnp.float32),
            sem, sem,
            sem((zn,)), sem((zn,)), sem((zn,)), sem((zn,)), sem((dp,)), sem((dp,)),
        ],
        compiler_params=pltpu.CompilerParams(collective_id=1, has_side_effects=True),
        name="mstep",
    )(pp, wt, wpart, mass, table)
    return (new_refs, ev[:, 0])


def solution(mesh):
    in_specs = (
        P(("groups", "dp"), None, None),
        P("dp", "groups", None),
        P(("groups", "dp")),
        P("groups"),
        P("groups"),
        P(),
    )
    out_specs = (P("dp", "groups", None), P(("groups", "dp")))
    return jax.shard_map(
        functools.partial(shards, mesh.shape["dp"]),
        mesh=mesh, in_specs=in_specs, out_specs=out_specs, check_vma=False,
    )
```

```python
import functools
import math

import jax
import jax.numpy as jnp
from jax import lax
from jax.experimental import pallas as pl
from jax.experimental.pallas import tpu as pltpu
from jax.sharding import PartitionSpec as P

R = 64
ROT = 36
HALF = ROT // 2
NC = HALF + 1
G = 32
MESH = pl.DeviceIdType.MESH
HIGHEST = lax.Precision.HIGHEST


def dev(index):
    return {"dp": index}


def ring_steps(zn):
    plus = zn // 2
    minus = zn - 1 - plus
    steps = []
    for d in range(1, plus + 1):
        steps.append((1, d))
        if d <= minus:
            steps.append((-1, d))
    return steps


def gather_kernel(zn, dp, window, refs_ref, part_ref, row_ref, focus_ref, cw_ref, prior_ref,
                  wt_ref, wpart_ref, table_ref, pp_ref, ev_ref, mass_ref,
                  out_ref, cres, energy, bias, psum, evcol, local_sem, send, recv, wsend, wrecv):
    me = lax.axis_index("dp")
    z, x, c = me // 4, (me // 2) % 2, me % 2
    flip_x = z * 4 + (1 - x) * 2 + c
    flip_c = z * 4 + x * 2 + (1 - c)
    n, m_all, q = part_ref.shape
    mb, k, _ = refs_ref.shape
    nall = n * dp
    steps = [(s, d) for d in range(1, zn) for s in (1, -1)]
    beside = {s: lax.rem(z + zn + s, zn) * 4 + x * 2 + c for s in (1, -1)}

    def holds(s, d):
        return z >= d if s == 1 else z + d < zn

    def goes(s):
        return z + 1 < zn if s == 1 else z >= 1

    def origin(s, d):
        return lax.rem(z + zn - s * d, zn) * 4

    barrier = pltpu.get_barrier_semaphore()
    greet = [beside[1], beside[-1], flip_x, flip_c]
    for p in greet:
        pl.semaphore_signal(barrier, inc=1, device_id=dev(p), device_id_type=MESH)
    pl.semaphore_wait(barrier, len(greet))

    count = 2 * (zn - 1)
    x0, c0 = count, 2 * count + 1

    def copy_of(src, block, target, slot):
        return pltpu.make_async_remote_copy(
            src_ref=src,
            dst_ref=out_ref.at[block],
            send_sem=send.at[slot],
            recv_sem=recv.at[slot],
            device_id=dev(target),
            device_id_type=MESH,
        )

    slot_of = {step: i for i, step in enumerate(steps)}
    for s in (1, -1):
        @pl.when(goes(s))
        def _():
            copy_of(refs_ref, me, beside[s], slot_of[(s, 1)]).start()
    copy_of(refs_ref, me, flip_x, x0).start()
    copy_of(refs_ref, me, flip_c, c0).start()
    keep = pltpu.make_async_copy(refs_ref, out_ref.at[me], local_sem)
    keep.start()

    lane = lax.broadcasted_iota(jnp.int32, (G, q), 1)
    radius = (jnp.where(lane < R, lane, lane - R).astype(jnp.float32) + 1.0) / R
    eye = lax.broadcasted_iota(jnp.int32, (G, G), 0) == lax.broadcasted_iota(jnp.int32, (G, G), 1)
    focus = jnp.sum(jnp.where(eye, jnp.broadcast_to(focus_ref[...], (G, G)), 0.0), axis=1, keepdims=True)
    phase = 20.0 * focus * (radius * radius)
    ctf = -(0.995 * jnp.sin(phase) + 0.1 * jnp.cos(phase))
    cw = jnp.concatenate([cw_ref[...], cw_ref[...]], axis=1)
    gain_table = cw * ctf
    power = gain_table * ctf

    def dot(a, b):
        return jnp.dot(a, b, precision=HIGHEST, preferred_element_type=jnp.float32)

    onehot = (row_ref[...] == lax.broadcasted_iota(jnp.int32, (G, n), 0)).astype(jnp.float32)

    def picked(table):
        return lax.dot_general(
            onehot, table, (((0,), (0,)), ((), ())),
            preferred_element_type=jnp.float32, precision=HIGHEST,
        )

    gain = picked(gain_table)
    anorm = 0.5 * picked(power)
    start = (me * (n * G)) // nall
    hot = (
        row_ref[...] == lax.broadcasted_iota(jnp.int32, (window, n), 0) + start
    ).astype(jnp.float32)
    below = lax.broadcasted_iota(jnp.int32, (window, G), 0) - lax.broadcasted_iota(jnp.int32, (window, G), 1)
    for d in range(dp):
        pick = (below == -(d * n * G // nall)).astype(jnp.float32)
        table_ref[d * window:(d + 1) * window, :] = dot(pick, power)

    chunk = 16

    @pl.loop(0, m_all // chunk)
    def _(i):
        at = pl.ds(pl.multiple_of(i * chunk, chunk), chunk)
        wide = part_ref[:, at, :].astype(jnp.float32) * gain[:, None, :]
        wt_ref[at] = jnp.swapaxes(wide, 0, 1).astype(jnp.bfloat16)

    wcopies = []
    for b in range(dp // 2):
        copy = pltpu.make_async_remote_copy(
            src_ref=wt_ref.at[pl.ds((2 * b + 1 - c) * mb, mb)],
            dst_ref=wpart_ref.at[b],
            send_sem=wsend.at[b],
            recv_sem=wrecv.at[b],
            device_id=dev(flip_c),
            device_id_type=MESH,
        )
        copy.start()
        wcopies.append(copy)

    cres[...] = jnp.zeros_like(cres)
    energy[...] = jnp.zeros_like(energy)
    lane_n = lax.broadcasted_iota(jnp.int32, (n, q), 1)
    sign = jnp.where(lane_n < R, jnp.float32(1.0), jnp.float32(-1.0))

    def products(block):
        @pl.loop(0, mb)
        def _(i):
            m = block * mb + i
            r = lax.rem(m, ROT)
            w = wt_ref[m]
            turned = (pltpu.roll(w.astype(jnp.float32), R, 1) * sign).astype(jnp.bfloat16)
            both = jnp.concatenate([w, turned], axis=0)
            ref = out_ref[block, i]
            cres[r] += lax.dot_general(
                both, ref, (((1,), (1,)), ((), ())), preferred_element_type=jnp.float32
            )
            wide = ref.astype(jnp.float32)
            energy[...] += wide * wide

    keep.wait()
    products(me)
    for i, (s, d) in enumerate(steps):
        @pl.when(holds(s, d))
        def _():
            block = origin(s, d) + x * 2 + c
            copy_of(out_ref.at[block], block, beside[s], slot_of[(s, d)]).wait_recv()
            if d + 1 < zn:
                @pl.when(goes(s))
                def _():
                    copy_of(out_ref.at[block], block, beside[s], slot_of[(s, d + 1)]).start()
            copy_of(out_ref.at[block], block, flip_x, x0 + 1 + i).start()
            copy_of(out_ref.at[block], block, flip_c, c0 + 1 + i).start()
            products(block)
    every = [(None, (1, 0))] + list(enumerate(steps))

    def guarded(s, d, body):
        if d == 0:
            body()
        else:
            pl.when(holds(s, d))(body)

    for i, (s, d) in every:
        j = 0 if i is None else i + 1

        def from_x(s=s, d=d, j=j):
            block = origin(s, d) + (1 - x) * 2 + c
            copy_of(out_ref.at[block], block, flip_x, x0 + j).wait_recv()
            copy_of(out_ref.at[block], block, flip_c, c0 + count + 1 + j).start()
            products(block)
            mine = origin(s, d) + x * 2 + (1 - c)
            copy_of(out_ref.at[mine], mine, flip_c, c0 + j).wait_recv()
            products(mine)

        guarded(s, d, from_x)
    for i, (s, d) in every:
        j = 0 if i is None else i + 1

        def from_core(s=s, d=d, j=j):
            block = origin(s, d) + (1 - x) * 2 + (1 - c)
            copy_of(out_ref.at[block], block, flip_c, c0 + count + 1 + j).wait_recv()
            products(block)

        guarded(s, d, from_core)

    scores_and_posterior(anorm, hot, prior_ref, pp_ref, ev_ref, mass_ref, cres, energy, bias, psum, evcol, n)

    for copy in wcopies:
        copy.wait()
    for i, (s, d) in every:
        j = 0 if i is None else i + 1

        def sent(s=s, d=d, j=j):
            block = origin(s, d) + x * 2 + c
            other = origin(s, d) + (1 - x) * 2 + c
            copy_of(out_ref.at[block], block, flip_x, x0 + j).wait_send()
            copy_of(out_ref.at[block], block, flip_c, c0 + j).wait_send()
            copy_of(out_ref.at[other], other, flip_c, c0 + count + 1 + j).wait_send()

        guarded(s, d, sent)
    for s in (1, -1):
        for d in range(0, zn - 1):
            room = jnp.minimum(z - d, zn - 2 - z) if s == 1 else jnp.minimum(zn - 1 - d - z, z - 1)

            @pl.when(room >= 0)
            def _():
                block = origin(s, d) + x * 2 + c
                copy_of(out_ref.at[block], block, beside[s], slot_of[(s, d + 1)]).wait_send()


def dft_even_odd(even_in, odd_in, use_cos):
    f = math.cos if use_cos else math.sin

    def one(items, j):
        total = None
        for i, v in items:
            w = f(2.0 * math.pi * ((i * j) % ROT) / ROT)
            if abs(w) < 1e-12:
                continue
            if abs(w - 1.0) < 1e-12:
                term = v
            elif abs(w + 1.0) < 1e-12:
                term = -v
            else:
                term = v * jnp.float32(w)
            total = term if total is None else total + term
        return total

    count = HALF // 2 + 1
    return [one(even_in, j) for j in range(count)], [one(odd_in, j) for j in range(count)]


def half_transform(values, use_cos):
    even = [(i, v) for i, v in values.items() if i % 2 == 0]
    odd = [(i, v) for i, v in values.items() if i % 2 == 1]
    es, os_ = dft_even_odd(even, odd, use_cos)
    zero = jnp.zeros_like(next(iter(values.values())))
    out = {}
    for j in range(HALF // 2 + 1):
        e = zero if es[j] is None else es[j]
        o = zero if os_[j] is None else os_[j]
        out[j] = e + o
        out[HALF - j] = (e - o) if use_cos else (o - e)
    return out


def scores_and_posterior(anorm, hot, prior_ref, pp_ref, ev_ref, mass_ref, cres, energy, bias, psum, evcol, n):
    norm = lax.dot_general(
        anorm, energy[...], (((1,), (1,)), ((), ())),
        preferred_element_type=jnp.float32, precision=HIGHEST,
    )
    bias[...] = jnp.log(prior_ref[...]) - norm

    rows = 16

    @pl.loop(0, n // rows)
    def _(i):
        at = pl.ds(pl.multiple_of(i * rows, rows), rows)
        at_im = pl.ds(pl.multiple_of(n + i * rows, rows), rows)
        a = {0: cres[0, at, :], HALF: cres[HALF, at, :]}
        b = {}
        for r in range(1, HALF):
            a[r] = cres[r, at, :] + cres[ROT - r, at, :]
            b[r] = cres[r, at_im, :] - cres[ROT - r, at_im, :]
        cosine = half_transform(a, True)
        sine = half_transform(b, False)
        add = bias[at, :]
        scores = {}
        for j in range(NC):
            base = cosine[j] + add
            if j in (0, HALF):
                scores[j] = base
            else:
                scores[j] = base - sine[j]
                scores[ROT - j] = base + sine[j]
        top = scores[0]
        for j in range(1, ROT):
            top = jnp.maximum(top, scores[j])
        top = jnp.max(top, axis=1, keepdims=True)
        total = None
        expo = {}
        for j in range(ROT):
            expo[j] = jnp.exp(scores[j] - top)
            total = expo[j] if total is None else total + expo[j]
        norm_total = jnp.sum(total, axis=1, keepdims=True)
        evcol[at, :] = jnp.broadcast_to(top + jnp.log(norm_total), (rows, n))
        inv = 1.0 / norm_total
        psum[at, :] = total * inv
        u = {0: expo[0] * inv, HALF: expo[HALF] * inv}
        v = {}
        for j in range(1, HALF):
            u[j] = (expo[j] + expo[ROT - j]) * inv
            v[j] = (expo[j] - expo[ROT - j]) * inv
        real = half_transform(u, True)
        imag = half_transform(v, False)
        for r in range(NC):
            pp_ref[r, at, :] = real[r].astype(jnp.bfloat16)
            pp_ref[NC + r, at, :] = imag[r].astype(jnp.bfloat16)

    square = (n, n)
    eye = lax.broadcasted_iota(jnp.int32, square, 0) == lax.broadcasted_iota(jnp.int32, square, 1)
    ev_ref[...] = jnp.sum(jnp.where(eye, evcol[...], 0.0), axis=0, keepdims=True)
    mass_ref[...] = lax.dot_general(
        hot, psum[...], (((1,), (0,)), ((), ())),
        preferred_element_type=jnp.float32, precision=HIGHEST,
    )


def mstep_kernel(zn, dp, pp_ref, wt_ref, wpart_ref, mass_ref, table_ref, out_ref,
                 pbuf, pt, xsend, xrecv, acc, zsend, zrecv, mslots,
                 psend_s, psend_r, xs, xr, zs, zr, ms, mr):
    me = lax.axis_index("dp")
    z, x, c = me // 4, (me // 2) % 2, me % 2
    flip_x = z * 4 + (1 - x) * 2 + c
    flip_c = z * 4 + x * 2 + (1 - c)
    mb, k, q = out_ref.shape

    barrier = pltpu.get_barrier_semaphore()
    for o in range(1, dp):
        pl.semaphore_signal(barrier, inc=1, device_id=dev(lax.rem(me + o, dp)), device_id_type=MESH)
    pl.semaphore_wait(barrier, dp - 1)

    pcopy = pltpu.make_async_remote_copy(
        src_ref=pp_ref, dst_ref=pbuf, send_sem=psend_s, recv_sem=psend_r,
        device_id=dev(flip_c), device_id_type=MESH,
    )
    pcopy.start()
    mcopies = []
    for o in range(1, dp):
        copy = pltpu.make_async_remote_copy(
            src_ref=mass_ref, dst_ref=mslots.at[me], send_sem=ms.at[o], recv_sem=mr.at[o],
            device_id=dev(lax.rem(me + o, dp)), device_id_type=MESH,
        )
        copy.start()
        mcopies.append(copy)
    mslots[me] = mass_ref[...]
    pcopy.wait()

    @pl.loop(0, 2 * NC)
    def _(i):
        pt[i] = jnp.concatenate([pp_ref[i], pbuf[i]], axis=0).T

    lane = lax.broadcasted_iota(jnp.int32, (k, q), 1)
    mask = jnp.where(lane < R, jnp.float32(-1.0), jnp.float32(1.0))

    def numer(zx, i):
        m = (zx * 2 + c) * mb + i
        r = lax.rem(m, ROT)
        rr = jnp.minimum(r, ROT - r)
        s = jnp.where(r > HALF, -1, 1).astype(jnp.float32)
        w = jnp.concatenate([wt_ref[m], wpart_ref[zx, i]], axis=0)
        u = jnp.dot(pt[rr], w, preferred_element_type=jnp.float32)
        v = jnp.dot(pt[NC + rr], w, preferred_element_type=jnp.float32)
        return u + pltpu.roll(v, R, 1) * (mask * s)

    steps = ring_steps(zn)
    reach = {1: zn // 2, -1: zn - 1 - zn // 2}
    order = [((s * (reach[s] + 1 - d)) % zn, s, d) for s, d in steps] + [(0, 0, 0)]
    xcopies = []
    for o, _, _ in order:
        zz = lax.rem(z + o, zn)

        @pl.loop(0, mb)
        def _(i):
            xsend[o, i] = numer(zz * 2 + 1 - x, i).astype(jnp.bfloat16)

        copy = pltpu.make_async_remote_copy(
            src_ref=xsend.at[o], dst_ref=xrecv.at[o], send_sem=xs.at[o], recv_sem=xr.at[o],
            device_id=dev(flip_x), device_id_type=MESH,
        )
        copy.start()
        xcopies.append(copy)

    zcopies = {}
    last = []
    for j, ((o, s, d), xcopy) in enumerate(zip(order, xcopies)):
        zz = lax.rem(z + o, zn)

        @pl.loop(0, mb)
        def _(i):
            acc[i] = numer(zz * 2 + x, i)

        xcopy.wait_recv()
        if o:
            before = None
            if d > 1:
                before, got = zcopies[(s, d - 1)]
                got.wait_recv()

            @pl.loop(0, mb)
            def _(i):
                total = acc[i] + xrecv[o, i].astype(jnp.float32)
                if before is not None:
                    total = total + zrecv[before, i].astype(jnp.float32)
                zsend[j, i] = total.astype(jnp.bfloat16)

            copy = pltpu.make_async_remote_copy(
                src_ref=zsend.at[j], dst_ref=zrecv.at[j], send_sem=zs.at[j], recv_sem=zr.at[j],
                device_id=dev(lax.rem(z + zn + s, zn) * 4 + x * 2 + c), device_id_type=MESH,
            )
            copy.start()
            zcopies[(s, d)] = (j, copy)
            if d == reach[s]:
                last.append((j, copy))
    for copy in mcopies:
        copy.wait_recv()
    wide = mslots[...].reshape(dp * mslots.shape[1], k)
    denom = 1.0 + lax.dot_general(
        wide, table_ref[...], (((0,), (0,)), ((), ())),
        preferred_element_type=jnp.float32, precision=HIGHEST,
    )
    inv = 1.0 / denom
    for _, copy in last:
        copy.wait_recv()

    @pl.loop(0, mb)
    def _(i):
        total = acc[i] + xrecv[0, i].astype(jnp.float32)
        for j, _ in last:
            total = total + zrecv[j, i].astype(jnp.float32)
        out_ref[i] = total * inv

    for copy in xcopies + [copy for _, copy in zcopies.values()] + mcopies:
        copy.wait_send()


def shards(dp, particles, refs, ctf_group, defocus, class_prior, cycle_weight):
    n, m_all, q = particles.shape
    mb, k, _ = refs.shape
    zn = dp // 4
    nall = n * dp
    window = -(-((n * G) // nall + 2) // 8) * 8

    vmem = pl.BlockSpec(memory_space=pltpu.VMEM)
    hbm = pl.BlockSpec(memory_space=pl.ANY)
    sem = pltpu.SemaphoreType.DMA
    copies = 8 * zn - 5
    wt, wpart, table, pp, ev, mass = pl.pallas_call(
        functools.partial(gather_kernel, zn, dp, window),
        out_shape=(
            jax.ShapeDtypeStruct((m_all, n, q), jnp.bfloat16),
            jax.ShapeDtypeStruct((dp // 2, mb, n, q), jnp.bfloat16),
            jax.ShapeDtypeStruct((dp * window, q), jnp.float32),
            jax.ShapeDtypeStruct((2 * NC, n, k), jnp.bfloat16),
            jax.ShapeDtypeStruct((1, n), jnp.float32),
            jax.ShapeDtypeStruct((window, k), jnp.float32),
        ),
        in_specs=[vmem] * 6,
        out_specs=(vmem, hbm, vmem, vmem, vmem, vmem),
        scratch_shapes=[
            pltpu.VMEM((dp, mb, k, q), jnp.bfloat16),
            pltpu.VMEM((ROT, 2 * n, k), jnp.float32),
            pltpu.VMEM((k, q), jnp.float32),
            pltpu.VMEM((n, k), jnp.float32),
            pltpu.VMEM((n, k), jnp.float32),
            pltpu.VMEM((n, n), jnp.float32),
            sem, sem((copies,)), sem((copies,)), sem((dp // 2,)), sem((dp // 2,)),
        ],
        compiler_params=pltpu.CompilerParams(collective_id=0, has_side_effects=True),
        name="gather",
    )(refs, particles, ctf_group[None, :], defocus[None, :], cycle_weight[None, :], class_prior[None, :])

    new_refs = pl.pallas_call(
        functools.partial(mstep_kernel, zn, dp),
        out_shape=jax.ShapeDtypeStruct((mb, k, q), jnp.float32),
        in_specs=[vmem] * 5,
        out_specs=vmem,
        scratch_shapes=[
            pltpu.VMEM((2 * NC, n, k), jnp.bfloat16),
            pltpu.VMEM((2 * NC, k, 2 * n), jnp.bfloat16),
            pltpu.VMEM((zn, mb, k, q), jnp.bfloat16),
            pltpu.VMEM((zn, mb, k, q), jnp.bfloat16),
            pltpu.VMEM((mb, k, q), jnp.float32),
            pltpu.VMEM((zn, mb, k, q), jnp.bfloat16),
            pltpu.VMEM((zn, mb, k, q), jnp.bfloat16),
            pltpu.VMEM((dp, window, k), jnp.float32),
            sem, sem,
            sem((zn,)), sem((zn,)), sem((zn,)), sem((zn,)), sem((dp,)), sem((dp,)),
        ],
        compiler_params=pltpu.CompilerParams(collective_id=1, has_side_effects=True),
        name="mstep",
    )(pp, wt, wpart, mass, table)
    return (new_refs, ev[0])


def solution(mesh):
    in_specs = (
        P(("groups", "dp"), None, None),
        P("dp", "groups", None),
        P(("groups", "dp")),
        P("groups"),
        P("groups"),
        P(),
    )
    out_specs = (P("dp", "groups", None), P(("groups", "dp")))
    return jax.shard_map(
        functools.partial(shards, mesh.shape["dp"]),
        mesh=mesh, in_specs=in_specs, out_specs=out_specs, check_vma=False,
    )
```

```python
import functools
import math

import jax
import jax.numpy as jnp
from jax import lax
from jax.experimental import pallas as pl
from jax.experimental.pallas import tpu as pltpu
from jax.sharding import PartitionSpec as P

R = 64
ROT = 36
HALF = ROT // 2
NC = HALF + 1
G = 32
MESH = pl.DeviceIdType.MESH
HIGHEST = lax.Precision.HIGHEST


def dev(index):
    return {"dp": index}


def ring_steps(zn):
    plus = zn // 2
    minus = zn - 1 - plus
    steps = []
    for d in range(1, plus + 1):
        steps.append((1, d))
        if d <= minus:
            steps.append((-1, d))
    return steps


def gather_kernel(zn, dp, window, refs_ref, part_ref, row_ref, focus_ref, cw_ref, prior_ref,
                  wt_ref, wpart_ref, table_ref, pp_ref, ev_ref, mass_ref,
                  out_ref, cres, energy, bias, psum, evcol, local_sem, send, recv, wsend, wrecv):
    me = lax.axis_index("dp")
    z, x, c = me // 4, (me // 2) % 2, me % 2
    flip_x = z * 4 + (1 - x) * 2 + c
    flip_c = z * 4 + x * 2 + (1 - c)
    n, m_all, q = part_ref.shape
    mb, k, _ = refs_ref.shape
    nall = n * dp
    steps = [(s, d) for d in range(1, zn) for s in (1, -1)]
    beside = {s: lax.rem(z + zn + s, zn) * 4 + x * 2 + c for s in (1, -1)}

    def holds(s, d):
        return z >= d if s == 1 else z + d < zn

    def goes(s):
        return z + 1 < zn if s == 1 else z >= 1

    def origin(s, d):
        return lax.rem(z + zn - s * d, zn) * 4

    barrier = pltpu.get_barrier_semaphore()
    greet = [beside[1], beside[-1], flip_x, flip_c]
    for p in greet:
        pl.semaphore_signal(barrier, inc=1, device_id=dev(p), device_id_type=MESH)
    pl.semaphore_wait(barrier, len(greet))

    count = 2 * (zn - 1)
    x0, c0 = count, 2 * count + 1

    def copy_of(src, block, target, slot):
        return pltpu.make_async_remote_copy(
            src_ref=src,
            dst_ref=out_ref.at[block],
            send_sem=send.at[slot],
            recv_sem=recv.at[slot],
            device_id=dev(target),
            device_id_type=MESH,
        )

    slot_of = {step: i for i, step in enumerate(steps)}
    for s in (1, -1):
        @pl.when(goes(s))
        def _():
            copy_of(refs_ref, me, beside[s], slot_of[(s, 1)]).start()
    copy_of(refs_ref, me, flip_x, x0).start()
    copy_of(refs_ref, me, flip_c, c0).start()
    keep = pltpu.make_async_copy(refs_ref, out_ref.at[me], local_sem)
    keep.start()

    lane = lax.broadcasted_iota(jnp.int32, (G, q), 1)
    radius = (jnp.where(lane < R, lane, lane - R).astype(jnp.float32) + 1.0) / R
    eye = lax.broadcasted_iota(jnp.int32, (G, G), 0) == lax.broadcasted_iota(jnp.int32, (G, G), 1)
    focus = jnp.sum(jnp.where(eye, jnp.broadcast_to(focus_ref[...], (G, G)), 0.0), axis=1, keepdims=True)
    phase = 20.0 * focus * (radius * radius)
    ctf = -(0.995 * jnp.sin(phase) + 0.1 * jnp.cos(phase))
    cw = jnp.concatenate([cw_ref[...], cw_ref[...]], axis=1)
    gain_table = cw * ctf
    power = gain_table * ctf

    def dot(a, b):
        return jnp.dot(a, b, precision=HIGHEST, preferred_element_type=jnp.float32)

    onehot = (row_ref[...] == lax.broadcasted_iota(jnp.int32, (G, n), 0)).astype(jnp.float32)

    def picked(table):
        return lax.dot_general(
            onehot, table, (((0,), (0,)), ((), ())),
            preferred_element_type=jnp.float32, precision=HIGHEST,
        )

    gain = picked(gain_table)
    anorm = 0.5 * picked(power)
    start = (me * (n * G)) // nall
    hot = (
        row_ref[...] == lax.broadcasted_iota(jnp.int32, (window, n), 0) + start
    ).astype(jnp.float32)
    below = lax.broadcasted_iota(jnp.int32, (window, G), 0) - lax.broadcasted_iota(jnp.int32, (window, G), 1)
    for d in range(dp):
        pick = (below == -(d * n * G // nall)).astype(jnp.float32)
        table_ref[d * window:(d + 1) * window, :] = dot(pick, power)

    chunk = 16

    @pl.loop(0, m_all // chunk)
    def _(i):
        at = pl.ds(pl.multiple_of(i * chunk, chunk), chunk)
        wide = part_ref[:, at, :].astype(jnp.float32) * gain[:, None, :]
        wt_ref[at] = jnp.swapaxes(wide, 0, 1).astype(jnp.bfloat16)

    wcopies = []
    for b in range(dp // 2):
        copy = pltpu.make_async_remote_copy(
            src_ref=wt_ref.at[pl.ds((2 * b + 1 - c) * mb, mb)],
            dst_ref=wpart_ref.at[b],
            send_sem=wsend.at[b],
            recv_sem=wrecv.at[b],
            device_id=dev(flip_c),
            device_id_type=MESH,
        )
        copy.start()
        wcopies.append(copy)

    cres[...] = jnp.zeros_like(cres)
    energy[...] = jnp.zeros_like(energy)
    lane_n = lax.broadcasted_iota(jnp.int32, (n, q), 1)
    sign = jnp.where(lane_n < R, jnp.float32(1.0), jnp.float32(-1.0))

    def products(block):
        @pl.loop(0, mb)
        def _(i):
            m = block * mb + i
            r = lax.rem(m, ROT)
            w = wt_ref[m]
            turned = (pltpu.roll(w.astype(jnp.float32), R, 1) * sign).astype(jnp.bfloat16)
            both = jnp.concatenate([w, turned], axis=0)
            ref = out_ref[block, i]
            cres[r] += lax.dot_general(
                both, ref, (((1,), (1,)), ((), ())), preferred_element_type=jnp.float32
            )
            wide = ref.astype(jnp.float32)
            energy[...] += wide * wide

    keep.wait()
    every = [(None, (1, 0))] + list(enumerate(steps))

    def guarded(s, d, body):
        if d == 0:
            body()
        else:
            pl.when(holds(s, d))(body)

    def from_x(j):
        s, d = every[j][1]

        def body():
            block = origin(s, d) + (1 - x) * 2 + c
            copy_of(out_ref.at[block], block, flip_x, x0 + j).wait_recv()
            copy_of(out_ref.at[block], block, flip_c, c0 + count + 1 + j).start()
            products(block)

        guarded(s, d, body)

    for i, (s, d) in enumerate(steps):
        @pl.when(holds(s, d))
        def _():
            block = origin(s, d) + x * 2 + c
            copy_of(out_ref.at[block], block, beside[s], slot_of[(s, d)]).wait_recv()
            if d + 1 < zn:
                @pl.when(goes(s))
                def _():
                    copy_of(out_ref.at[block], block, beside[s], slot_of[(s, d + 1)]).start()
            copy_of(out_ref.at[block], block, flip_x, x0 + 1 + i).start()
            copy_of(out_ref.at[block], block, flip_c, c0 + 1 + i).start()
            if i > 1:
                products(block)
        if i == 1:
            products(me)
            for late, (s1, d1) in enumerate(steps[:2]):
                @pl.when(holds(s1, d1))
                def _():
                    products(origin(s1, d1) + x * 2 + c)
        if i >= 1:
            from_x(i - 1)
    from_x(len(steps) - 1)
    from_x(len(steps))
    for half in (x, 1 - x):
        for j, (_, (s, d)) in enumerate(every):
            slot = c0 + j + (0 if half is x else count + 1)

            def from_core(s=s, d=d, slot=slot, half=half):
                block = origin(s, d) + half * 2 + (1 - c)
                copy_of(out_ref.at[block], block, flip_c, slot).wait_recv()
                products(block)

            guarded(s, d, from_core)

    scores_and_posterior(anorm, hot, prior_ref, pp_ref, ev_ref, mass_ref, cres, energy, bias, psum, evcol, n)

    for copy in wcopies:
        copy.wait()
    for i, (s, d) in every:
        j = 0 if i is None else i + 1

        def sent(s=s, d=d, j=j):
            block = origin(s, d) + x * 2 + c
            other = origin(s, d) + (1 - x) * 2 + c
            copy_of(out_ref.at[block], block, flip_x, x0 + j).wait_send()
            copy_of(out_ref.at[block], block, flip_c, c0 + j).wait_send()
            copy_of(out_ref.at[other], other, flip_c, c0 + count + 1 + j).wait_send()

        guarded(s, d, sent)
    for s in (1, -1):
        for d in range(0, zn - 1):
            room = jnp.minimum(z - d, zn - 2 - z) if s == 1 else jnp.minimum(zn - 1 - d - z, z - 1)

            @pl.when(room >= 0)
            def _():
                block = origin(s, d) + x * 2 + c
                copy_of(out_ref.at[block], block, beside[s], slot_of[(s, d + 1)]).wait_send()


def dft_even_odd(even_in, odd_in, use_cos):
    f = math.cos if use_cos else math.sin

    def one(items, j):
        total = None
        for i, v in items:
            w = f(2.0 * math.pi * ((i * j) % ROT) / ROT)
            if abs(w) < 1e-12:
                continue
            if abs(w - 1.0) < 1e-12:
                term = v
            elif abs(w + 1.0) < 1e-12:
                term = -v
            else:
                term = v * jnp.float32(w)
            total = term if total is None else total + term
        return total

    count = HALF // 2 + 1
    return [one(even_in, j) for j in range(count)], [one(odd_in, j) for j in range(count)]


def half_transform(values, use_cos):
    even = [(i, v) for i, v in values.items() if i % 2 == 0]
    odd = [(i, v) for i, v in values.items() if i % 2 == 1]
    es, os_ = dft_even_odd(even, odd, use_cos)
    zero = jnp.zeros_like(next(iter(values.values())))
    out = {}
    for j in range(HALF // 2 + 1):
        e = zero if es[j] is None else es[j]
        o = zero if os_[j] is None else os_[j]
        out[j] = e + o
        out[HALF - j] = (e - o) if use_cos else (o - e)
    return out


def scores_and_posterior(anorm, hot, prior_ref, pp_ref, ev_ref, mass_ref, cres, energy, bias, psum, evcol, n):
    norm = lax.dot_general(
        anorm, energy[...], (((1,), (1,)), ((), ())),
        preferred_element_type=jnp.float32, precision=HIGHEST,
    )
    bias[...] = jnp.log(prior_ref[...]) - norm

    rows = 16

    @pl.loop(0, n // rows)
    def _(i):
        at = pl.ds(pl.multiple_of(i * rows, rows), rows)
        at_im = pl.ds(pl.multiple_of(n + i * rows, rows), rows)
        a = {0: cres[0, at, :], HALF: cres[HALF, at, :]}
        b = {}
        for r in range(1, HALF):
            a[r] = cres[r, at, :] + cres[ROT - r, at, :]
            b[r] = cres[r, at_im, :] - cres[ROT - r, at_im, :]
        cosine = half_transform(a, True)
        sine = half_transform(b, False)
        add = bias[at, :]
        scores = {}
        for j in range(NC):
            base = cosine[j] + add
            if j in (0, HALF):
                scores[j] = base
            else:
                scores[j] = base - sine[j]
                scores[ROT - j] = base + sine[j]
        top = scores[0]
        for j in range(1, ROT):
            top = jnp.maximum(top, scores[j])
        top = jnp.max(top, axis=1, keepdims=True)
        total = None
        expo = {}
        for j in range(ROT):
            expo[j] = jnp.exp(scores[j] - top)
            total = expo[j] if total is None else total + expo[j]
        norm_total = jnp.sum(total, axis=1, keepdims=True)
        evcol[at, :] = jnp.broadcast_to(top + jnp.log(norm_total), (rows, n))
        inv = 1.0 / norm_total
        psum[at, :] = total * inv
        u = {0: expo[0] * inv, HALF: expo[HALF] * inv}
        v = {}
        for j in range(1, HALF):
            u[j] = (expo[j] + expo[ROT - j]) * inv
            v[j] = (expo[j] - expo[ROT - j]) * inv
        real = half_transform(u, True)
        imag = half_transform(v, False)
        for r in range(NC):
            pp_ref[r, at, :] = real[r].astype(jnp.bfloat16)
            pp_ref[NC + r, at, :] = imag[r].astype(jnp.bfloat16)

    square = (n, n)
    eye = lax.broadcasted_iota(jnp.int32, square, 0) == lax.broadcasted_iota(jnp.int32, square, 1)
    ev_ref[...] = jnp.sum(jnp.where(eye, evcol[...], 0.0), axis=0, keepdims=True)
    mass_ref[...] = lax.dot_general(
        hot, psum[...], (((1,), (0,)), ((), ())),
        preferred_element_type=jnp.float32, precision=HIGHEST,
    )


def mstep_kernel(zn, dp, pp_ref, wt_ref, wpart_ref, mass_ref, table_ref, out_ref,
                 pbuf, pt, xsend, xrecv, acc, zsend, zrecv, mslots,
                 psend_s, psend_r, xs, xr, zs, zr, ms, mr):
    me = lax.axis_index("dp")
    z, x, c = me // 4, (me // 2) % 2, me % 2
    flip_x = z * 4 + (1 - x) * 2 + c
    flip_c = z * 4 + x * 2 + (1 - c)
    mb, k, q = out_ref.shape

    barrier = pltpu.get_barrier_semaphore()
    for o in range(1, dp):
        pl.semaphore_signal(barrier, inc=1, device_id=dev(lax.rem(me + o, dp)), device_id_type=MESH)
    pl.semaphore_wait(barrier, dp - 1)

    pcopy = pltpu.make_async_remote_copy(
        src_ref=pp_ref, dst_ref=pbuf, send_sem=psend_s, recv_sem=psend_r,
        device_id=dev(flip_c), device_id_type=MESH,
    )
    pcopy.start()
    mcopies = []
    for o in range(1, dp):
        copy = pltpu.make_async_remote_copy(
            src_ref=mass_ref, dst_ref=mslots.at[me], send_sem=ms.at[o], recv_sem=mr.at[o],
            device_id=dev(lax.rem(me + o, dp)), device_id_type=MESH,
        )
        copy.start()
        mcopies.append(copy)
    mslots[me] = mass_ref[...]
    pcopy.wait()

    @pl.loop(0, 2 * NC)
    def _(i):
        pt[i] = jnp.concatenate([pp_ref[i], pbuf[i]], axis=0).T

    lane = lax.broadcasted_iota(jnp.int32, (k, q), 1)
    mask = jnp.where(lane < R, jnp.float32(-1.0), jnp.float32(1.0))

    def numer(zx, i):
        m = (zx * 2 + c) * mb + i
        r = lax.rem(m, ROT)
        rr = jnp.minimum(r, ROT - r)
        s = jnp.where(r > HALF, -1, 1).astype(jnp.float32)
        w = jnp.concatenate([wt_ref[m], wpart_ref[zx, i]], axis=0)
        u = jnp.dot(pt[rr], w, preferred_element_type=jnp.float32)
        v = jnp.dot(pt[NC + rr], w, preferred_element_type=jnp.float32)
        return u + pltpu.roll(v, R, 1) * (mask * s)

    steps = ring_steps(zn)
    reach = {1: zn // 2, -1: zn - 1 - zn // 2}
    order = [((s * (reach[s] + 1 - d)) % zn, s, d) for s, d in steps] + [(0, 0, 0)]
    xcopies = []
    for o, _, _ in order:
        zz = lax.rem(z + o, zn)

        @pl.loop(0, mb)
        def _(i):
            xsend[o, i] = numer(zz * 2 + 1 - x, i).astype(jnp.bfloat16)

        copy = pltpu.make_async_remote_copy(
            src_ref=xsend.at[o], dst_ref=xrecv.at[o], send_sem=xs.at[o], recv_sem=xr.at[o],
            device_id=dev(flip_x), device_id_type=MESH,
        )
        copy.start()
        xcopies.append(copy)

    zcopies = {}
    last = []
    for j, ((o, s, d), xcopy) in enumerate(zip(order, xcopies)):
        zz = lax.rem(z + o, zn)

        @pl.loop(0, mb)
        def _(i):
            acc[i] = numer(zz * 2 + x, i)

        xcopy.wait_recv()
        if o:
            before = None
            if d > 1:
                before, got = zcopies[(s, d - 1)]
                got.wait_recv()

            @pl.loop(0, mb)
            def _(i):
                total = acc[i] + xrecv[o, i].astype(jnp.float32)
                if before is not None:
                    total = total + zrecv[before, i].astype(jnp.float32)
                zsend[j, i] = total.astype(jnp.bfloat16)

            copy = pltpu.make_async_remote_copy(
                src_ref=zsend.at[j], dst_ref=zrecv.at[j], send_sem=zs.at[j], recv_sem=zr.at[j],
                device_id=dev(lax.rem(z + zn + s, zn) * 4 + x * 2 + c), device_id_type=MESH,
            )
            copy.start()
            zcopies[(s, d)] = (j, copy)
            if d == reach[s]:
                last.append((j, copy))
    for copy in mcopies:
        copy.wait_recv()
    wide = mslots[...].reshape(dp * mslots.shape[1], k)
    denom = 1.0 + lax.dot_general(
        wide, table_ref[...], (((0,), (0,)), ((), ())),
        preferred_element_type=jnp.float32, precision=HIGHEST,
    )
    inv = 1.0 / denom
    for _, copy in last:
        copy.wait_recv()

    @pl.loop(0, mb)
    def _(i):
        total = acc[i] + xrecv[0, i].astype(jnp.float32)
        for j, _ in last:
            total = total + zrecv[j, i].astype(jnp.float32)
        out_ref[i] = total * inv

    for copy in xcopies + [copy for _, copy in zcopies.values()] + mcopies:
        copy.wait_send()


def shards(dp, particles, refs, ctf_group, defocus, class_prior, cycle_weight):
    n, m_all, q = particles.shape
    mb, k, _ = refs.shape
    zn = dp // 4
    nall = n * dp
    window = -(-((n * G) // nall + 2) // 8) * 8

    vmem = pl.BlockSpec(memory_space=pltpu.VMEM)
    hbm = pl.BlockSpec(memory_space=pl.ANY)
    sem = pltpu.SemaphoreType.DMA
    copies = 8 * zn - 5
    wt, wpart, table, pp, ev, mass = pl.pallas_call(
        functools.partial(gather_kernel, zn, dp, window),
        out_shape=(
            jax.ShapeDtypeStruct((m_all, n, q), jnp.bfloat16),
            jax.ShapeDtypeStruct((dp // 2, mb, n, q), jnp.bfloat16),
            jax.ShapeDtypeStruct((dp * window, q), jnp.float32),
            jax.ShapeDtypeStruct((2 * NC, n, k), jnp.bfloat16),
            jax.ShapeDtypeStruct((1, n), jnp.float32),
            jax.ShapeDtypeStruct((window, k), jnp.float32),
        ),
        in_specs=[vmem] * 6,
        out_specs=(vmem, hbm, vmem, vmem, vmem, vmem),
        scratch_shapes=[
            pltpu.VMEM((dp, mb, k, q), jnp.bfloat16),
            pltpu.VMEM((ROT, 2 * n, k), jnp.float32),
            pltpu.VMEM((k, q), jnp.float32),
            pltpu.VMEM((n, k), jnp.float32),
            pltpu.VMEM((n, k), jnp.float32),
            pltpu.VMEM((n, n), jnp.float32),
            sem, sem((copies,)), sem((copies,)), sem((dp // 2,)), sem((dp // 2,)),
        ],
        compiler_params=pltpu.CompilerParams(collective_id=0, has_side_effects=True),
        name="gather",
    )(refs, particles, ctf_group[None, :], defocus[None, :], cycle_weight[None, :], class_prior[None, :])

    new_refs = pl.pallas_call(
        functools.partial(mstep_kernel, zn, dp),
        out_shape=jax.ShapeDtypeStruct((mb, k, q), jnp.float32),
        in_specs=[vmem] * 5,
        out_specs=vmem,
        scratch_shapes=[
            pltpu.VMEM((2 * NC, n, k), jnp.bfloat16),
            pltpu.VMEM((2 * NC, k, 2 * n), jnp.bfloat16),
            pltpu.VMEM((zn, mb, k, q), jnp.bfloat16),
            pltpu.VMEM((zn, mb, k, q), jnp.bfloat16),
            pltpu.VMEM((mb, k, q), jnp.float32),
            pltpu.VMEM((zn, mb, k, q), jnp.bfloat16),
            pltpu.VMEM((zn, mb, k, q), jnp.bfloat16),
            pltpu.VMEM((dp, window, k), jnp.float32),
            sem, sem,
            sem((zn,)), sem((zn,)), sem((zn,)), sem((zn,)), sem((dp,)), sem((dp,)),
        ],
        compiler_params=pltpu.CompilerParams(collective_id=1, has_side_effects=True),
        name="mstep",
    )(pp, wt, wpart, mass, table)
    return (new_refs, ev[0])


def solution(mesh):
    in_specs = (
        P(("groups", "dp"), None, None),
        P("dp", "groups", None),
        P(("groups", "dp")),
        P("groups"),
        P("groups"),
        P(),
    )
    out_specs = (P("dp", "groups", None), P(("groups", "dp")))
    return jax.shard_map(
        functools.partial(shards, mesh.shape["dp"]),
        mesh=mesh, in_specs=in_specs, out_specs=out_specs, check_vma=False,
    )
```
